32 devices in a mesh: gx: 4 (over x, core), gy: 8 (over z, y).
Axes of the slice: x: 2, y: 2, z: 4, core: 2. Of those that a mesh axis runs over, the one named last changes fastest.
Arguments:
- velocity: float32 [16, 384, 8192], P(None, 'gy', 'gx'), may hold values from -8 to 8
- blend_left: float32 [128, 10], replicated, may hold values from -2 to 2
- blend_right: float32 [128, 10], replicated, may hold values from -2 to 2
- injection: float32 [16], replicated, may hold values from 0.5 to 2
Outputs:
- dudx: float32 [16, 384, 8192], P(None, 'gy', 'gx')
- rhs: float32 [16, 384, 8192], P(None, 'gy', 'gx')
The draws below stay inside these ranges and needn't reach their ends.
All inputs are finite; a program needn't handle non-finite values.
Results may differ from the reference program's by a relative error of at most 0.000086.
Values sent between devices are 32-bit elements; how exact they have to be, the bound alone decides.
A program may use at most 128 MiB of HBM per device.

```python
import math
import jax
import jax.numpy as jnp
from jax import lax

NX = 8192
CONT = 128
DEND = 10
ZP = 16
NY = 384


def draw_velocity(key, part):
    xs = jnp.arange(NX, dtype=jnp.float32) / NX
    ys = jnp.arange(NY, dtype=jnp.float32) / NY
    spread = xs[None, None, :] + ys[None, :, None]
    scale = 0.5 * 10.0 ** (0.25 * spread)
    noise = jnp.clip(jax.random.normal(key, (ZP, NY, NX), jnp.float32), -5.0, 5.0)
    return (scale * noise).astype(jnp.float32)


def gaussian(rng, extent, deviation, bound, kind=jnp.bfloat16):
    entries = deviation * jax.random.normal(rng, extent, jnp.float32)
    return jnp.clip(entries, min=-bound, max=bound).astype(kind)


def setup_inputs(seed: int = 0) -> dict:
    key_of = jax.random.split(jax.random.key(seed), 5)
    velocity = draw_velocity(jax.random.fold_in(key_of[4], 71), 0)
    blend_left = gaussian(key_of[1], (CONT, DEND), DEND ** -0.5, 2.0, jnp.float32)
    blend_right = gaussian(key_of[2], (CONT, DEND), DEND ** -0.5, 2.0, jnp.float32)
    injection = jnp.clip(jnp.exp(jax.random.uniform(key_of[3], (ZP,), jnp.float32, math.log(0.5), math.log(2.0))), 0.5, 2.0)
    return dict(velocity=velocity, blend_left=blend_left, blend_right=blend_right, injection=injection)


TWO_PI = 2.0 * math.pi
ALPHA = 36.0
ORDER = 36


def filter_factor(period):
    freq = jnp.arange(period, dtype=jnp.int32)
    half = period // 2
    signed = jnp.where(freq < half, freq, freq - period).astype(jnp.float32)
    ratio = jnp.abs(signed) / half
    value = (TWO_PI / period) * signed * jnp.exp(-ALPHA * ratio ** ORDER)
    return jnp.where(freq == half, jnp.zeros_like(value), value)


def reference(velocity, blend_left, blend_right, injection):
    period = NX + CONT
    factor = filter_factor(period)
    high = lax.Precision.HIGHEST

    def plane_derivative(plane):
        left = plane[:, :DEND]
        right = plane[:, NX - DEND:]
        cont = jnp.dot(left, blend_left.T, precision=high) + jnp.dot(right, blend_right.T, precision=high)
        ext = jnp.concatenate([plane, cont], axis=1)
        spec = jnp.fft.fft(ext, axis=-1)
        deriv = jnp.fft.ifft(spec * (1j * factor), axis=-1).real
        return deriv[:, :NX].astype(jnp.float32)

    dudx = lax.map(plane_derivative, velocity)
    energy = jnp.mean(velocity * velocity, axis=(1, 2))
    forcing = injection / energy
    rhs = -velocity * dudx + forcing[:, None, None] * velocity
    return dudx, rhs
```

```python
import functools

import jax
import jax.numpy as jnp
import numpy as np
from jax import lax
from jax.experimental import pallas as pl
from jax.experimental.pallas import tpu as pltpu
from jax.sharding import PartitionSpec as P

ALPHA = 36.0
ORDER = 36
BLOCK = 256
PACK = 16
HIGH = lax.Precision.HIGHEST


def taps(period):
    freq = np.arange(period)
    half = period // 2
    signed = np.where(freq < half, freq, freq - period).astype(np.float64)
    factor = 2.0 * np.pi / period * signed * np.exp(-ALPHA * (np.abs(signed) / half) ** ORDER)
    factor[half] = 0.0
    return np.fft.ifft(1j * factor).real


def toeplitz(period, reach):
    kernel = taps(period)
    source = np.arange(BLOCK + 2 * reach)[:, None] - reach
    target = np.arange(BLOCK)[None, :]
    table = kernel[(target - source) % period]
    high = table.astype(np.float32).astype(jnp.bfloat16)
    low = (table - high.astype(np.float64)).astype(np.float32).astype(jnp.bfloat16)
    return high, low


def exchange_kernel(
    nx, ny, v_ref, bl_ref, br_ref, left_ref, right_ref, total_ref,
    vbuf, xbuf, ybuf, part, ends, blend, cont,
    load_sem, xsend, xrecv, ysend, yrecv, hsend, hrecv, esend, erecv, csem,
):
    planes, rows, width = v_ref.shape
    reach = left_ref.shape[2]
    depth = bl_ref.shape[1]
    gx = lax.axis_index("gx")
    gy = lax.axis_index("gy")
    first = gx == 0
    last = gx == nx - 1

    def load(p):
        return pltpu.make_async_copy(v_ref.at[p], vbuf.at[p], load_sem.at[p])

    def start_load(p, carry):
        load(p).start()
        return carry

    lax.fori_loop(0, planes, start_load, 0)

    barrier = pltpu.get_barrier_semaphore()
    for d in range(1, nx):
        pl.semaphore_signal(barrier, inc=1, device_id={"gx": lax.rem(gx + d, nx)})
    for d in range(1, ny):
        pl.semaphore_signal(barrier, inc=1, device_id={"gy": lax.rem(gy + d, ny)})
    pl.semaphore_wait(barrier, nx + ny - 2)

    to_right = pltpu.make_async_remote_copy(
        src_ref=v_ref.at[:, :, pl.ds(width - reach, reach)],
        dst_ref=left_ref,
        send_sem=hsend.at[0],
        recv_sem=hrecv.at[0],
        device_id={"gx": lax.rem(gx + 1, nx)},
    )
    to_left = pltpu.make_async_remote_copy(
        src_ref=v_ref.at[:, :, pl.ds(0, reach)],
        dst_ref=right_ref,
        send_sem=hsend.at[1],
        recv_sem=hrecv.at[1],
        device_id={"gx": lax.rem(gx + nx - 1, nx)},
    )

    @pl.when(jnp.logical_not(last))
    def _():
        to_right.start()

    @pl.when(jnp.logical_not(first))
    def _():
        to_left.start()

    def plane_sum(p, carry):
        load(p).wait()
        x = vbuf[p]
        s = jnp.sum((x * x).reshape(rows // 8, 8, width), axis=0)
        acc = s[:, 0:128]
        for c in range(1, width // 128):
            acc = acc + s[:, c * 128 : (c + 1) * 128]
        part[pl.ds(p, 1), :] = jnp.sum(acc, axis=0, keepdims=True)
        return carry

    lax.fori_loop(0, planes, plane_sum, 0)

    xcopies = []
    for d in range(1, nx):
        copy = pltpu.make_async_remote_copy(
            src_ref=part,
            dst_ref=xbuf.at[d],
            send_sem=xsend.at[d],
            recv_sem=xrecv.at[d],
            device_id={"gx": lax.rem(gx + d, nx)},
        )
        copy.start()
        xcopies.append(copy)

    sel_row = lax.broadcasted_iota(jnp.int32, (PACK, reach), 0)
    sel_col = lax.broadcasted_iota(jnp.int32, (PACK, reach), 1)

    def pack(lane, offset):
        pick = jnp.where((sel_row < depth) & (sel_col == sel_row + offset), 1.0, 0.0)
        tile = vbuf[:, :, lane : lane + reach].reshape(planes * rows, reach)
        return lax.dot_general(
            pick.astype(jnp.float32), tile, (((1,), (1,)), ((), ())), precision=HIGH
        )

    ends_out = pltpu.make_async_remote_copy(
        src_ref=ends.at[0], dst_ref=ends.at[0], send_sem=esend.at[0],
        recv_sem=erecv.at[0], device_id={"gx": nx - 1},
    )
    ends_back = pltpu.make_async_remote_copy(
        src_ref=ends.at[1], dst_ref=ends.at[1], send_sem=esend.at[1],
        recv_sem=erecv.at[1], device_id={"gx": 0},
    )

    @pl.when(first)
    def _():
        ends[0] = pack(0, 0)
        ends_out.start()

    @pl.when(last)
    def _():
        ends[1] = pack(width - reach, reach - depth)
        ends_back.start()

    for copy in xcopies:
        copy.wait()
    mine = part[...]
    for d in range(1, nx):
        mine = mine + xbuf[d]
    ybuf[0] = mine
    ycopies = []
    for d in range(1, ny):
        copy = pltpu.make_async_remote_copy(
            src_ref=ybuf.at[0],
            dst_ref=ybuf.at[d],
            send_sem=ysend.at[d],
            recv_sem=yrecv.at[d],
            device_id={"gy": lax.rem(gy + d, ny)},
        )
        copy.start()
        ycopies.append(copy)

    def continuation():
        blend[...] = jnp.zeros_like(blend)
        blend[0, :, 0:depth] = bl_ref[...]
        blend[1, :, 0:depth] = br_ref[...]
        turned = jnp.dot(blend[0], ends[0], precision=HIGH) + jnp.dot(
            blend[1], ends[1], precision=HIGH
        )
        cont[...] = jnp.transpose(turned).reshape(cont.shape)

    @pl.when(first)
    def _():
        ends_out.wait_send()
        ends_back.wait_recv()
        continuation()
        out = pltpu.make_async_copy(cont, left_ref, csem)
        out.start()
        out.wait()

    @pl.when(last)
    def _():
        ends_back.wait_send()
        ends_out.wait_recv()
        continuation()
        out = pltpu.make_async_copy(cont, right_ref, csem)
        out.start()
        out.wait()

    for copy in ycopies:
        copy.wait()
    every = ybuf[0]
    for d in range(1, ny):
        every = every + ybuf[d]
    total_ref[...] = every

    @pl.when(jnp.logical_not(last))
    def _():
        to_right.wait_send()
        to_left.wait_recv()

    @pl.when(jnp.logical_not(first))
    def _():
        to_left.wait_send()
        to_right.wait_recv()


def exchange(velocity, blend_left, blend_right, nx, ny):
    planes, rows, width = velocity.shape
    reach = blend_left.shape[0]
    halo = jax.ShapeDtypeStruct((planes, rows, reach), jnp.float32)
    dma = pltpu.SemaphoreType.DMA
    return pl.pallas_call(
        functools.partial(exchange_kernel, nx, ny),
        out_shape=(halo, halo, jax.ShapeDtypeStruct((planes, 128), jnp.float32)),
        in_specs=[
            pl.BlockSpec(memory_space=pl.ANY),
            pl.BlockSpec(memory_space=pltpu.VMEM),
            pl.BlockSpec(memory_space=pltpu.VMEM),
        ],
        out_specs=(
            pl.BlockSpec(memory_space=pl.ANY),
            pl.BlockSpec(memory_space=pl.ANY),
            pl.BlockSpec(memory_space=pltpu.VMEM),
        ),
        scratch_shapes=[
            pltpu.VMEM((planes, rows, width), jnp.float32),
            pltpu.VMEM((nx, planes, 128), jnp.float32),
            pltpu.VMEM((ny, planes, 128), jnp.float32),
            pltpu.VMEM((planes, 128), jnp.float32),
            pltpu.VMEM((2, PACK, planes * rows), jnp.float32),
            pltpu.VMEM((2, reach, PACK), jnp.float32),
            pltpu.VMEM((planes, rows, reach), jnp.float32),
            dma((planes,)),
            dma((nx,)),
            dma((nx,)),
            dma((ny,)),
            dma((ny,)),
            dma((2,)),
            dma((2,)),
            dma((2,)),
            dma((2,)),
            dma,
        ],
        compiler_params=pltpu.CompilerParams(
            collective_id=0, has_side_effects=True, vmem_limit_bytes=48 * 2**20
        ),
        name="exchange",
    )(velocity, blend_left, blend_right)


def filter_kernel(
    count, v_ref, left_ref, right_ref, high_ref, low_ref, total_ref, inj_ref,
    dudx_ref, rhs_ref, ehigh, elow,
):
    group, rows, width = v_ref.shape
    reach = left_ref.shape[2]
    lines = group * rows
    blocks = width // BLOCK

    def put(c, lane, x):
        x = x.reshape(lines, x.shape[2])
        high = x.astype(jnp.bfloat16)
        low = (x - high.astype(jnp.float32)).astype(jnp.bfloat16)
        spot = (pl.ds(c * lines, lines), pl.ds(lane, x.shape[1]))
        ehigh[spot] = high
        elow[spot] = low

    put(0, 0, left_ref[...])
    put(0, reach, v_ref[:, :, 0 : BLOCK - reach])
    for c in range(1, blocks):
        put(c, 0, v_ref[:, :, c * BLOCK - reach : (c + 1) * BLOCK - reach])
    put(blocks, 0, v_ref[:, :, width - reach :])
    put(blocks, reach, right_ref[...])

    step = pl.program_id(0)
    forcing = []
    for g in range(group):
        p = step * group + g
        energy = jnp.sum(total_ref[pl.ds(p, 1), :], axis=1, keepdims=True) / count
        forcing.append(inj_ref[p] / energy)

    chunk = min(4, blocks)
    for c0 in range(0, blocks, chunk):
        here = pl.ds(c0 * lines, chunk * lines)
        there = pl.ds((c0 + 1) * lines, chunk * lines)
        wide_high = jnp.concatenate([ehigh[here, :], ehigh[there, :]], axis=1)
        wide_low = jnp.concatenate([elow[here, :], elow[there, :]], axis=1)
        dot = functools.partial(jnp.dot, preferred_element_type=jnp.float32)
        res = dot(wide_high, high_ref[...])
        res = res + dot(wide_low, high_ref[...])
        res = res + dot(wide_high, low_ref[...])
        res = res.reshape(chunk, group, rows, BLOCK)
        for i in range(chunk):
            lane = (c0 + i) * BLOCK
            for g in range(group):
                d = res[i, g]
                dudx_ref[g, :, lane : lane + BLOCK] = d
                rhs_ref[g, :, lane : lane + BLOCK] = v_ref[g, :, lane : lane + BLOCK] * (
                    forcing[g] - d
                )


def apply_filter(velocity, left, right, total, injection, period, count):
    planes, rows, width = velocity.shape
    reach = left.shape[2]
    high, low = toeplitz(period, reach)
    group = min(4, planes)
    lines = group * rows
    blocks = width // BLOCK
    whole = jax.ShapeDtypeStruct(velocity.shape, jnp.float32)
    by_plane = lambda i: (i, 0, 0)
    fixed = lambda i: (0, 0)
    return pl.pallas_call(
        functools.partial(filter_kernel, count),
        grid=(planes // group,),
        out_shape=(whole, whole),
        in_specs=[
            pl.BlockSpec((group, rows, width), by_plane),
            pl.BlockSpec((group, rows, reach), by_plane),
            pl.BlockSpec((group, rows, reach), by_plane),
            pl.BlockSpec(high.shape, fixed),
            pl.BlockSpec(low.shape, fixed),
            pl.BlockSpec(total.shape, fixed),
            pl.BlockSpec(memory_space=pltpu.SMEM),
        ],
        out_specs=(
            pl.BlockSpec((group, rows, width), by_plane),
            pl.BlockSpec((group, rows, width), by_plane),
        ),
        scratch_shapes=[
            pltpu.VMEM(((blocks + 1) * lines, BLOCK), jnp.bfloat16),
            pltpu.VMEM(((blocks + 1) * lines, BLOCK), jnp.bfloat16),
        ],
        compiler_params=pltpu.CompilerParams(vmem_limit_bytes=56 * 2**20),
        name="filter",
    )(velocity, left, right, jnp.asarray(high), jnp.asarray(low), total, injection)


def per_device(nx, ny, velocity, blend_left, blend_right, injection):
    planes, rows, width = velocity.shape
    period = width * nx + blend_left.shape[0]
    count = width * nx * rows * ny
    left, right, total = exchange(velocity, blend_left, blend_right, nx, ny)
    return apply_filter(velocity, left, right, total, injection, period, count)


def solution(mesh):
    placed = (P(None, "gy", "gx"), P(), P(), P())
    return jax.shard_map(
        functools.partial(per_device, mesh.shape["gx"], mesh.shape["gy"]),
        mesh=mesh,
        in_specs=placed,
        out_specs=(P(None, "gy", "gx"), P(None, "gy", "gx")),
        check_vma=False,
    )
```

```python
import functools

import jax
import jax.numpy as jnp
import numpy as np
from jax import lax
from jax.experimental import pallas as pl
from jax.experimental.pallas import tpu as pltpu
from jax.sharding import PartitionSpec as P

ALPHA = 36.0
ORDER = 36
BLOCK = 256
PACK = 16
HIGH = lax.Precision.HIGHEST


def taps(period):
    freq = np.arange(period)
    half = period // 2
    signed = np.where(freq < half, freq, freq - period).astype(np.float64)
    factor = 2.0 * np.pi / period * signed * np.exp(-ALPHA * (np.abs(signed) / half) ** ORDER)
    factor[half] = 0.0
    return np.fft.ifft(1j * factor).real


def toeplitz(period, reach):
    kernel = taps(period)
    source = np.arange(BLOCK + 2 * reach)[:, None] - reach
    target = np.arange(BLOCK)[None, :]
    table = kernel[(target - source) % period]
    high = table.astype(np.float32).astype(jnp.bfloat16)
    low = (table - high.astype(np.float64)).astype(np.float32).astype(jnp.bfloat16)
    return high, low


def split(x):
    high = x.astype(jnp.bfloat16)
    return high, (x - high.astype(jnp.float32)).astype(jnp.bfloat16)


def exchange_kernel(
    nx, ny, v_ref, bl_ref, br_ref, table_ref, left_ref, right_ref, total_ref, vbuf, inner_ref,
    ehigh, elow, table, xbuf, ybuf, part, ends, blend,
    load_sem, xsend, xrecv, ysend, yrecv, hsend, hrecv, esend, erecv, tsem,
):
    planes, rows, width = v_ref.shape
    reach = left_ref.shape[2]
    depth = bl_ref.shape[0]
    blocks = width // BLOCK
    group = min(4, planes)
    lines = group * rows
    gx = lax.axis_index("gx")
    gy = lax.axis_index("gy")
    first = gx == 0
    last = gx == nx - 1

    def load(p):
        return pltpu.make_async_copy(v_ref.at[p], vbuf.at[p], load_sem.at[p])

    def start_load(p, carry):
        load(p).start()
        return carry

    lax.fori_loop(0, planes, start_load, 0)
    load_table = pltpu.make_async_copy(table_ref, table, tsem)
    load_table.start()

    barrier = pltpu.get_barrier_semaphore()
    for d in range(1, nx):
        pl.semaphore_signal(barrier, inc=1, device_id={"gx": lax.rem(gx + d, nx)})
    for d in range(1, ny):
        pl.semaphore_signal(barrier, inc=1, device_id={"gy": lax.rem(gy + d, ny)})
    pl.semaphore_wait(barrier, nx + ny - 2)

    to_right = pltpu.make_async_remote_copy(
        src_ref=v_ref.at[:, :, pl.ds(width - reach, reach)],
        dst_ref=left_ref,
        send_sem=hsend.at[0],
        recv_sem=hrecv.at[0],
        device_id={"gx": lax.rem(gx + 1, nx)},
    )
    to_left = pltpu.make_async_remote_copy(
        src_ref=v_ref.at[:, :, pl.ds(0, reach)],
        dst_ref=right_ref,
        send_sem=hsend.at[1],
        recv_sem=hrecv.at[1],
        device_id={"gx": lax.rem(gx + nx - 1, nx)},
    )

    @pl.when(jnp.logical_not(last))
    def _():
        to_right.start()

    @pl.when(jnp.logical_not(first))
    def _():
        to_left.start()

    def plane_sum(p, carry):
        load(p).wait()
        x = vbuf[p]
        s = jnp.sum((x * x).reshape(rows // 8, 8, width), axis=0)
        acc = s[:, 0:128]
        for c in range(1, width // 128):
            acc = acc + s[:, c * 128 : (c + 1) * 128]
        part[pl.ds(p, 1), :] = jnp.sum(acc, axis=0, keepdims=True)
        return carry

    lax.fori_loop(0, planes, plane_sum, 0)

    xcopies = []
    for d in range(1, nx):
        copy = pltpu.make_async_remote_copy(
            src_ref=part,
            dst_ref=xbuf.at[d],
            send_sem=xsend.at[d],
            recv_sem=xrecv.at[d],
            device_id={"gx": lax.rem(gx + d, nx)},
        )
        copy.start()
        xcopies.append(copy)

    sel_row = lax.broadcasted_iota(jnp.int32, (PACK, reach), 0)
    sel_col = lax.broadcasted_iota(jnp.int32, (PACK, reach), 1)

    def pack(lane, offset):
        pick = jnp.where((sel_row < depth) & (sel_col == sel_row + offset), 1.0, 0.0)
        tile = vbuf[:, :, lane : lane + reach].reshape(planes * rows, reach)
        return lax.dot_general(
            pick.astype(jnp.float32), tile, (((1,), (1,)), ((), ())), precision=HIGH
        )

    ends_out = pltpu.make_async_remote_copy(
        src_ref=ends.at[0], dst_ref=ends.at[0], send_sem=esend.at[0],
        recv_sem=erecv.at[0], device_id={"gx": nx - 1},
    )
    ends_back = pltpu.make_async_remote_copy(
        src_ref=ends.at[1], dst_ref=ends.at[1], send_sem=esend.at[1],
        recv_sem=erecv.at[1], device_id={"gx": 0},
    )

    @pl.when(first)
    def _():
        ends[0] = pack(0, 0)
        ends_out.start()

    @pl.when(last)
    def _():
        ends[1] = pack(width - reach, reach - depth)
        ends_back.start()

    ehigh[0:lines, 0:reach] = jnp.zeros((lines, reach), jnp.bfloat16)
    elow[0:lines, 0:reach] = jnp.zeros((lines, reach), jnp.bfloat16)
    tail = (pl.ds(blocks * lines, lines), pl.ds(BLOCK - reach, reach))
    ehigh[tail] = jnp.zeros((lines, reach), jnp.bfloat16)
    elow[tail] = jnp.zeros((lines, reach), jnp.bfloat16)

    def put(c, lane, x):
        high, low = split(x.reshape(lines, x.shape[2]))
        spot = (pl.ds(c * lines, lines), pl.ds(lane, x.shape[2]))
        ehigh[spot] = high
        elow[spot] = low

    def inner(step, carry):
        these = pl.ds(step * group, group)
        put(0, reach, vbuf[these, :, 0 : BLOCK - reach])
        for c in range(1, blocks):
            put(c, 0, vbuf[these, :, c * BLOCK - reach : (c + 1) * BLOCK - reach])
        put(blocks, 0, vbuf[these, :, width - reach : width])
        chunk = min(4, blocks)
        for c0 in range(0, blocks, chunk):
            here = pl.ds(c0 * lines, chunk * lines)
            there = pl.ds((c0 + 1) * lines, chunk * lines)
            h0, h1 = ehigh[here, :], ehigh[there, :]
            wide = jnp.concatenate([h0, h1, elow[here, :], elow[there, :], h0, h1], axis=1)
            res = jnp.dot(wide, table[...], preferred_element_type=jnp.float32)
            res = res.reshape(chunk, group, rows, BLOCK)
            for i in range(chunk):
                lane = (c0 + i) * BLOCK
                inner_ref[these, :, lane : lane + BLOCK] = res[i]
        return carry

    load_table.wait()
    inner(0, 0)

    for copy in xcopies:
        copy.wait()
    mine = part[...]
    for d in range(1, nx):
        mine = mine + xbuf[d]
    ybuf[0] = mine
    ycopies = []
    for d in range(1, ny):
        copy = pltpu.make_async_remote_copy(
            src_ref=ybuf.at[0],
            dst_ref=ybuf.at[d],
            send_sem=ysend.at[d],
            recv_sem=yrecv.at[d],
            device_id={"gy": lax.rem(gy + d, ny)},
        )
        copy.start()
        ycopies.append(copy)

    lax.fori_loop(1, planes // group, inner, 0)

    def continuation(halo_ref):
        blend[...] = jnp.zeros_like(blend)
        blend[0, 0:depth, :] = bl_ref[...]
        blend[1, 0:depth, :] = br_ref[...]
        mixed = lax.dot_general(
            ends[...].reshape(2 * PACK, planes * rows),
            blend[...].reshape(2 * PACK, reach),
            (((0,), (0,)), ((), ())),
            precision=HIGH,
        )
        halo_ref[...] = mixed.reshape(halo_ref.shape)

    @pl.when(first)
    def _():
        ends_out.wait_send()
        ends_back.wait_recv()
        continuation(left_ref)

    @pl.when(last)
    def _():
        ends_back.wait_send()
        ends_out.wait_recv()
        continuation(right_ref)

    for copy in ycopies:
        copy.wait()
    every = ybuf[0]
    for d in range(1, ny):
        every = every + ybuf[d]
    total_ref[...] = every

    @pl.when(jnp.logical_not(last))
    def _():
        to_right.wait_send()
        to_left.wait_recv()

    @pl.when(jnp.logical_not(first))
    def _():
        to_left.wait_send()
        to_right.wait_recv()


def exchange(velocity, blend_left, blend_right, table, nx, ny):
    planes, rows, width = velocity.shape
    reach = blend_left.shape[0]
    group = min(4, planes)
    lines = group * rows
    blocks = width // BLOCK
    halo = jax.ShapeDtypeStruct((planes, rows, reach), jnp.float32)
    whole = jax.ShapeDtypeStruct(velocity.shape, jnp.float32)
    dma = pltpu.SemaphoreType.DMA
    vmem = pl.BlockSpec(memory_space=pltpu.VMEM)
    hbm = pl.BlockSpec(memory_space=pltpu.HBM)
    return pl.pallas_call(
        functools.partial(exchange_kernel, nx, ny),
        out_shape=(halo, halo, jax.ShapeDtypeStruct((planes, 128), jnp.float32), whole, whole),
        in_specs=[hbm, vmem, vmem, hbm],
        out_specs=(vmem, vmem, vmem, vmem, vmem),
        scratch_shapes=[
            pltpu.VMEM(((blocks + 1) * lines, BLOCK), jnp.bfloat16),
            pltpu.VMEM(((blocks + 1) * lines, BLOCK), jnp.bfloat16),
            pltpu.VMEM(table.shape, table.dtype),
            pltpu.VMEM((nx, planes, 128), jnp.float32),
            pltpu.VMEM((ny, planes, 128), jnp.float32),
            pltpu.VMEM((planes, 128), jnp.float32),
            pltpu.VMEM((2, PACK, planes * rows), jnp.float32),
            pltpu.VMEM((2, PACK, reach), jnp.float32),
            dma((planes,)),
            dma((nx,)),
            dma((nx,)),
            dma((ny,)),
            dma((ny,)),
            dma((2,)),
            dma((2,)),
            dma((2,)),
            dma((2,)),
            dma,
        ],
        compiler_params=pltpu.CompilerParams(
            collective_id=0, has_side_effects=True, vmem_limit_bytes=38 * 2**20
        ),
        name="exchange",
    )(velocity, blend_left.T, blend_right.T, table)


def finish_kernel(
    count, left_ref, right_ref, tleft_ref, tright_ref, total_ref, inj_ref, v_ref, inner_ref,
    dudx_ref, rhs_ref,
):
    group, rows, width = dudx_ref.shape
    reach = left_ref.shape[2]
    lines = group * rows
    step = pl.program_id(0)
    these = pl.ds(step * group, group)

    def edge(halo_ref, weight_ref):
        high, low = split(halo_ref[these].reshape(lines, reach))
        wide = jnp.concatenate([high, low, high], axis=1)
        res = jnp.dot(wide, weight_ref[...], preferred_element_type=jnp.float32)
        return res.reshape(group, rows, reach)

    from_left = edge(left_ref, tleft_ref)
    from_right = edge(right_ref, tright_ref)
    for g in range(group):
        p = step * group + g
        energy = jnp.sum(total_ref[pl.ds(p, 1), :], axis=1, keepdims=True) / count
        forcing = inj_ref[p] / energy
        for lane in range(0, width, reach):
            spot = pl.ds(lane, reach)
            d = inner_ref[p, :, spot]
            if lane == 0:
                d = d + from_left[g]
            if lane == width - reach:
                d = d + from_right[g]
            dudx_ref[g, :, spot] = d
            rhs_ref[g, :, spot] = v_ref[p, :, spot] * (forcing - d)


def finish(velocity, inner, left, right, total, injection, tleft, tright, count):
    planes, rows, width = velocity.shape
    group = min(2, planes)
    whole = jax.ShapeDtypeStruct(velocity.shape, jnp.float32)
    vmem = pl.BlockSpec(memory_space=pltpu.VMEM)
    part = pl.BlockSpec((group, rows, width), lambda i: (i, 0, 0))
    return pl.pallas_call(
        functools.partial(finish_kernel, count),
        grid=(planes // group,),
        out_shape=(whole, whole),
        in_specs=[vmem] * 5 + [pl.BlockSpec(memory_space=pltpu.SMEM)] + [vmem] * 2,
        out_specs=(part, part),
        compiler_params=pltpu.CompilerParams(vmem_limit_bytes=32 * 2**20),
        name="finish",
    )(left, right, tleft, tright, total, injection, velocity, inner)


def per_device(nx, ny, velocity, blend_left, blend_right, injection):
    planes, rows, width = velocity.shape
    reach = blend_left.shape[0]
    period = width * nx + reach
    count = width * nx * rows * ny
    high, low = toeplitz(period, reach)
    table = jnp.asarray(np.concatenate([high, high, low], axis=0))
    head, foot = slice(0, reach), slice(BLOCK + reach, None)
    near, far = slice(0, reach), slice(BLOCK - reach, None)
    tleft = jnp.asarray(np.concatenate([high[head, near], high[head, near], low[head, near]]))
    tright = jnp.asarray(np.concatenate([high[foot, far], high[foot, far], low[foot, far]]))
    left, right, total, points, inner = exchange(
        velocity, blend_left, blend_right, table, nx, ny
    )
    return finish(points, inner, left, right, total, injection, tleft, tright, count)


def solution(mesh):
    placed = (P(None, "gy", "gx"), P(), P(), P())
    return jax.shard_map(
        functools.partial(per_device, mesh.shape["gx"], mesh.shape["gy"]),
        mesh=mesh,
        in_specs=placed,
        out_specs=(P(None, "gy", "gx"), P(None, "gy", "gx")),
        check_vma=False,
    )
```

```python
import functools

import jax
import jax.numpy as jnp
import numpy as np
from jax import lax
from jax.experimental import pallas as pl
from jax.experimental.pallas import tpu as pltpu
from jax.sharding import PartitionSpec as P

ALPHA = 36.0
ORDER = 36
BLOCK = 256
PACK = 16
HIGH = lax.Precision.HIGHEST


def taps(period):
    freq = np.arange(period)
    half = period // 2
    signed = np.where(freq < half, freq, freq - period).astype(np.float64)
    factor = 2.0 * np.pi / period * signed * np.exp(-ALPHA * (np.abs(signed) / half) ** ORDER)
    factor[half] = 0.0
    return np.fft.ifft(1j * factor).real


def toeplitz(period, reach):
    kernel = taps(period)
    source = np.arange(BLOCK + 2 * reach)[:, None] - reach
    target = np.arange(BLOCK)[None, :]
    table = kernel[(target - source) % period]
    high = table.astype(np.float32).astype(jnp.bfloat16)
    low = (table - high.astype(np.float64)).astype(np.float32).astype(jnp.bfloat16)
    return high, low


def split(x):
    high = x.astype(jnp.bfloat16)
    return high, (x - high.astype(jnp.float32)).astype(jnp.bfloat16)


def exchange_kernel(
    nx, ny, depth, v_ref, table_ref, left_ref, right_ref, ends, total_ref, vbuf, inner_ref,
    ehigh, elow, table, sums, part,
    load_sem, ssend, srecv, hsend, hrecv, esend, erecv, tsem,
):
    planes, rows, width = v_ref.shape
    reach = left_ref.shape[2]
    blocks = width // BLOCK
    group = min(4, planes)
    lines = group * rows
    gx = lax.axis_index("gx")
    gy = lax.axis_index("gy")
    first = gx == 0
    last = gx == nx - 1

    def load(p):
        return pltpu.make_async_copy(v_ref.at[p], vbuf.at[p], load_sem.at[p])

    def start_load(p, carry):
        load(p).start()
        return carry

    lax.fori_loop(0, planes, start_load, 0)
    deep = BLOCK + 2 * reach
    table_loads = [
        pltpu.make_async_copy(
            table_ref.at[pl.ds(source * deep, deep), :],
            table.at[pl.ds(i * deep, deep), :],
            tsem.at[i],
        )
        for i, source in enumerate((0, 0, 1))
    ]
    for copy in table_loads:
        copy.start()

    barrier = pltpu.get_barrier_semaphore()

    def partner(d):
        return {
            "gx": lax.rem(gx + d // ny, nx),
            "gy": lax.rem(gy + lax.rem(d, ny), ny),
        }

    def greet(d, carry):
        pl.semaphore_signal(barrier, inc=1, device_id=partner(d))
        return carry

    lax.fori_loop(1, nx * ny, greet, 0)
    pl.semaphore_wait(barrier, nx * ny - 1)

    to_right = pltpu.make_async_remote_copy(
        src_ref=v_ref.at[:, :, pl.ds(width - reach, reach)],
        dst_ref=left_ref,
        send_sem=hsend.at[0],
        recv_sem=hrecv.at[0],
        device_id={"gx": lax.rem(gx + 1, nx)},
    )
    to_left = pltpu.make_async_remote_copy(
        src_ref=v_ref.at[:, :, pl.ds(0, reach)],
        dst_ref=right_ref,
        send_sem=hsend.at[1],
        recv_sem=hrecv.at[1],
        device_id={"gx": lax.rem(gx + nx - 1, nx)},
    )

    @pl.when(jnp.logical_not(last))
    def _():
        to_right.start()

    @pl.when(jnp.logical_not(first))
    def _():
        to_left.start()

    def plane_sum(p, carry):
        load(p).wait()
        x = vbuf[p]
        s = jnp.sum((x * x).reshape(rows // 8, 8, width), axis=0)
        acc = s[:, 0:128]
        for c in range(1, width // 128):
            acc = acc + s[:, c * 128 : (c + 1) * 128]
        part[pl.ds(p, 1), :] = jnp.sum(acc, axis=0, keepdims=True)
        return carry

    lax.fori_loop(0, planes, plane_sum, 0)

    row = lax.dot_general(
        jnp.ones((8, 128), jnp.float32), part[...], (((1,), (1,)), ((), ())), precision=HIGH
    )
    sums[0] = jnp.zeros((1, 128), jnp.float32)
    sums[0, :, 0:planes] = row[0:1]

    def give(d, carry):
        pltpu.make_async_remote_copy(
            src_ref=sums.at[0],
            dst_ref=sums.at[d],
            send_sem=ssend,
            recv_sem=srecv,
            device_id=partner(d),
        ).start()
        return carry

    lax.fori_loop(1, nx * ny, give, 0)

    sel_row = lax.broadcasted_iota(jnp.int32, (PACK, reach), 0)
    sel_col = lax.broadcasted_iota(jnp.int32, (PACK, reach), 1)

    def pack(lane, offset):
        pick = jnp.where((sel_row < depth) & (sel_col == sel_row + offset), 1.0, 0.0)
        tile = vbuf[:, :, lane : lane + reach].reshape(planes * rows, reach)
        return lax.dot_general(
            pick.astype(jnp.float32), tile, (((1,), (1,)), ((), ())), precision=HIGH
        )

    ends_out = pltpu.make_async_remote_copy(
        src_ref=ends.at[0], dst_ref=ends.at[0], send_sem=esend.at[0],
        recv_sem=erecv.at[0], device_id={"gx": nx - 1},
    )
    ends_back = pltpu.make_async_remote_copy(
        src_ref=ends.at[1], dst_ref=ends.at[1], send_sem=esend.at[1],
        recv_sem=erecv.at[1], device_id={"gx": 0},
    )

    @pl.when(first)
    def _():
        ends[0] = pack(0, 0)
        ends_out.start()

    @pl.when(last)
    def _():
        ends[1] = pack(width - reach, reach - depth)
        ends_back.start()

    ehigh[0:lines, 0:reach] = jnp.zeros((lines, reach), jnp.bfloat16)
    elow[0:lines, 0:reach] = jnp.zeros((lines, reach), jnp.bfloat16)
    tail = (pl.ds(blocks * lines, lines), pl.ds(BLOCK - reach, reach))
    ehigh[tail] = jnp.zeros((lines, reach), jnp.bfloat16)
    elow[tail] = jnp.zeros((lines, reach), jnp.bfloat16)

    def put(c, lane, x):
        high, low = split(x.reshape(lines, x.shape[2]))
        spot = (pl.ds(c * lines, lines), pl.ds(lane, x.shape[2]))
        ehigh[spot] = high
        elow[spot] = low

    def inner(step, carry):
        these = pl.ds(step * group, group)
        put(0, reach, vbuf[these, :, 0 : BLOCK - reach])
        for c in range(1, blocks):
            put(c, 0, vbuf[these, :, c * BLOCK - reach : (c + 1) * BLOCK - reach])
        put(blocks, 0, vbuf[these, :, width - reach : width])
        chunk = min(4, blocks)
        for c0 in range(0, blocks, chunk):
            here = pl.ds(c0 * lines, chunk * lines)
            there = pl.ds((c0 + 1) * lines, chunk * lines)
            h0, h1 = ehigh[here, :], ehigh[there, :]
            wide = jnp.concatenate([h0, h1, elow[here, :], elow[there, :], h0, h1], axis=1)
            res = jnp.dot(wide, table[...], preferred_element_type=jnp.float32)
            res = res.reshape(chunk, group, rows, BLOCK)
            for i in range(chunk):
                lane = (c0 + i) * BLOCK
                inner_ref[these, :, lane : lane + BLOCK] = res[i]
        return carry

    for copy in table_loads:
        copy.wait()
    lax.fori_loop(0, planes // group, inner, 0)

    @pl.when(first)
    def _():
        ends_out.wait_send()
        ends_back.wait_recv()

    @pl.when(last)
    def _():
        ends_back.wait_send()
        ends_out.wait_recv()

    others = sums.at[pl.ds(1, nx * ny - 1)]
    pltpu.make_async_copy(others, others, ssend).wait()
    pltpu.make_async_copy(others, others, srecv).wait()
    total_ref[...] = jnp.sum(sums[...], axis=0)

    @pl.when(jnp.logical_not(last))
    def _():
        to_right.wait_send()
        to_left.wait_recv()

    @pl.when(jnp.logical_not(first))
    def _():
        to_left.wait_send()
        to_right.wait_recv()


def exchange(velocity, table, reach, depth, nx, ny):
    planes, rows, width = velocity.shape
    group = min(4, planes)
    lines = group * rows
    blocks = width // BLOCK
    halo = jax.ShapeDtypeStruct((planes, rows, reach), jnp.float32)
    ends = jax.ShapeDtypeStruct((2, PACK, planes * rows), jnp.float32)
    total = jax.ShapeDtypeStruct((1, 128), jnp.float32)
    whole = jax.ShapeDtypeStruct(velocity.shape, jnp.float32)
    dma = pltpu.SemaphoreType.DMA
    vmem = pl.BlockSpec(memory_space=pltpu.VMEM)
    hbm = pl.BlockSpec(memory_space=pltpu.HBM)
    return pl.pallas_call(
        functools.partial(exchange_kernel, nx, ny, depth),
        out_shape=(halo, halo, ends, total, whole, whole),
        in_specs=[hbm, hbm],
        out_specs=(vmem,) * 6,
        scratch_shapes=[
            pltpu.VMEM(((blocks + 1) * lines, BLOCK), jnp.bfloat16),
            pltpu.VMEM(((blocks + 1) * lines, BLOCK), jnp.bfloat16),
            pltpu.VMEM((3 * (BLOCK + 2 * reach), BLOCK), table.dtype),
            pltpu.VMEM((nx * ny, 1, 128), jnp.float32),
            pltpu.VMEM((planes, 128), jnp.float32),
            dma((planes,)),
            dma,
            dma,
            dma((2,)),
            dma((2,)),
            dma((2,)),
            dma((2,)),
            dma((3,)),
        ],
        compiler_params=pltpu.CompilerParams(
            collective_id=0, has_side_effects=True, vmem_limit_bytes=38 * 2**20
        ),
        name="exchange",
    )(velocity, table)


def finish_kernel(
    nx, count, left_ref, right_ref, ends_ref, bl_ref, br_ref, tleft_ref, tright_ref,
    total_ref, inj_ref, v_ref, inner_ref, dudx_ref, rhs_ref,
    halo, blend, near, far, rbuf, isem, nsem, rsem,
):
    planes, rows, width = v_ref.shape
    reach = left_ref.shape[2]
    depth = bl_ref.shape[0]
    lines = planes * rows
    gx = lax.axis_index("gx")
    middle = pl.ds(reach, width - 2 * reach)

    def inside(p):
        return pltpu.make_async_copy(
            inner_ref.at[p, :, middle], dudx_ref.at[p, :, middle], isem.at[p]
        )

    for p in range(planes):
        inside(p).start()

    def continuation():
        blend[...] = jnp.zeros_like(blend)
        blend[0, 0:depth, :] = bl_ref[...]
        blend[1, 0:depth, :] = br_ref[...]
        return lax.dot_general(
            ends_ref[...].reshape(2 * PACK, lines),
            blend[...].reshape(2 * PACK, reach),
            (((0,), (0,)), ((), ())),
            precision=HIGH,
        )

    def edge(halo_ref, own, weight_ref, lane, result):
        @pl.when(own)
        def _():
            halo[...] = continuation()

        @pl.when(jnp.logical_not(own))
        def _():
            halo[...] = halo_ref[...].reshape(lines, reach)

        high, low = split(halo[...])
        wide = jnp.concatenate([high, low, high], axis=1)
        res = jnp.dot(wide, weight_ref[...], preferred_element_type=jnp.float32)
        result[...] = inner_ref[:, :, lane : lane + reach] + res.reshape(planes, rows, reach)

    edge(left_ref, gx == 0, tleft_ref, 0, near)
    put_near = pltpu.make_async_copy(near, dudx_ref.at[:, :, pl.ds(0, reach)], nsem.at[0])
    put_near.start()
    edge(right_ref, gx == nx - 1, tright_ref, width - reach, far)
    put_far = pltpu.make_async_copy(
        far, dudx_ref.at[:, :, pl.ds(width - reach, reach)], nsem.at[1]
    )
    put_far.start()

    place = lax.broadcasted_iota(jnp.int32, (1, 128), 1)
    total = total_ref[...]

    def put_rhs(p):
        return pltpu.make_async_copy(rbuf.at[p], rhs_ref.at[p], rsem.at[p])

    def plane(p, carry):
        here = jnp.sum(jnp.where(place == p, total, 0.0), axis=1, keepdims=True)
        forcing = inj_ref[p] / (here / count)
        low, high = pl.ds(0, reach), pl.ds(width - reach, reach)
        rbuf[p, :, low] = v_ref[p, :, low] * (forcing - near[p])
        rbuf[p, :, middle] = v_ref[p, :, middle] * (forcing - inner_ref[p, :, middle])
        rbuf[p, :, high] = v_ref[p, :, high] * (forcing - far[p])
        put_rhs(p).start()
        return carry

    lax.fori_loop(0, planes, plane, 0)
    for p in range(planes):
        inside(p).wait()
    put_near.wait()
    put_far.wait()
    for p in range(planes):
        put_rhs(p).wait()


def finish(nx, count, velocity, inner, left, right, ends, blends, total, injection, tables):
    planes, rows, width = velocity.shape
    reach = left.shape[2]
    whole = jax.ShapeDtypeStruct(velocity.shape, jnp.float32)
    vmem = pl.BlockSpec(memory_space=pltpu.VMEM)
    hbm = pl.BlockSpec(memory_space=pltpu.HBM)
    dma = pltpu.SemaphoreType.DMA
    strip = pltpu.VMEM((planes, rows, reach), jnp.float32)
    return pl.pallas_call(
        functools.partial(finish_kernel, nx, count),
        out_shape=(whole, whole),
        in_specs=[vmem] * 8 + [pl.BlockSpec(memory_space=pltpu.SMEM)] + [vmem] * 2,
        out_specs=(hbm, hbm),
        scratch_shapes=[
            pltpu.VMEM((planes * rows, reach), jnp.float32),
            pltpu.VMEM((2, PACK, reach), jnp.float32),
            strip,
            strip,
            pltpu.VMEM(velocity.shape, jnp.float32),
            dma((planes,)),
            dma((2,)),
            dma((planes,)),
        ],
        compiler_params=pltpu.CompilerParams(vmem_limit_bytes=36 * 2**20),
        name="finish",
    )(left, right, ends, *blends, *tables, total, injection, velocity, inner)


def per_device(nx, ny, velocity, blend_left, blend_right, injection):
    planes, rows, width = velocity.shape
    reach = blend_left.shape[0]
    period = width * nx + reach
    count = width * nx * rows * ny
    high, low = toeplitz(period, reach)
    table = jnp.asarray(np.concatenate([high, low], axis=0))
    head, foot = slice(0, reach), slice(BLOCK + reach, None)
    near, far = slice(0, reach), slice(BLOCK - reach, None)
    tleft = jnp.asarray(np.concatenate([high[head, near], high[head, near], low[head, near]]))
    tright = jnp.asarray(np.concatenate([high[foot, far], high[foot, far], low[foot, far]]))
    left, right, ends, total, points, inner = exchange(
        velocity, table, reach, blend_left.shape[1], nx, ny
    )
    blends = (blend_left.T, blend_right.T)
    return finish(
        nx, count, points, inner, left, right, ends, blends, total, injection, (tleft, tright)
    )


def solution(mesh):
    placed = (P(None, "gy", "gx"), P(), P(), P())
    return jax.shard_map(
        functools.partial(per_device, mesh.shape["gx"], mesh.shape["gy"]),
        mesh=mesh,
        in_specs=placed,
        out_specs=(P(None, "gy", "gx"), P(None, "gy", "gx")),
        check_vma=False,
    )
```

```python
import functools

import jax
import jax.numpy as jnp
import numpy as np
from jax import lax
from jax.experimental import pallas as pl
from jax.experimental.pallas import tpu as pltpu
from jax.sharding import PartitionSpec as P

ALPHA = 36.0
ORDER = 36
BLOCK = 256
PACK = 16
HIGH = lax.Precision.HIGHEST


def taps(period):
    freq = np.arange(period)
    half = period // 2
    signed = np.where(freq < half, freq, freq - period).astype(np.float64)
    factor = 2.0 * np.pi / period * signed * np.exp(-ALPHA * (np.abs(signed) / half) ** ORDER)
    factor[half] = 0.0
    return np.fft.ifft(1j * factor).real


def toeplitz(period, reach):
    kernel = taps(period)
    source = np.arange(BLOCK + 2 * reach)[:, None] - reach
    target = np.arange(BLOCK)[None, :]
    table = kernel[(target - source) % period]
    high = table.astype(np.float32).astype(jnp.bfloat16)
    low = (table - high.astype(np.float64)).astype(np.float32).astype(jnp.bfloat16)
    return high, low


def split(x):
    high = x.astype(jnp.bfloat16)
    return high, (x - high.astype(jnp.float32)).astype(jnp.bfloat16)


def exchange_kernel(
    nx, ny, depth, v_ref, table_ref, left_ref, right_ref, ends, total_ref, vbuf, inner_ref,
    ehigh, elow, table, sums, part,
    load_sem, ssend, srecv, hsend, hrecv, esend, erecv, tsem,
):
    planes, rows, width = v_ref.shape
    reach = left_ref.shape[2]
    blocks = width // BLOCK
    group = min(4, planes)
    lines = group * rows
    gx = lax.axis_index("gx")
    gy = lax.axis_index("gy")
    first = gx == 0
    last = gx == nx - 1

    def load(p):
        return pltpu.make_async_copy(v_ref.at[p], vbuf.at[p], load_sem.at[p])

    def start_load(p, carry):
        load(p).start()
        return carry

    lax.fori_loop(0, planes, start_load, 0)
    deep = BLOCK + 2 * reach
    table_loads = [
        pltpu.make_async_copy(
            table_ref.at[pl.ds(source * deep, deep), :],
            table.at[pl.ds(i * deep, deep), :],
            tsem.at[i],
        )
        for i, source in enumerate((0, 0, 1))
    ]
    for copy in table_loads:
        copy.start()

    barrier = pltpu.get_barrier_semaphore()

    def partner(d):
        return {
            "gx": lax.rem(gx + d // ny, nx),
            "gy": lax.rem(gy + lax.rem(d, ny), ny),
        }

    def greet(d, carry):
        pl.semaphore_signal(barrier, inc=1, device_id=partner(d))
        return carry

    lax.fori_loop(1, nx * ny, greet, 0)
    ehigh[0:lines, 0:reach] = jnp.zeros((lines, reach), jnp.bfloat16)
    elow[0:lines, 0:reach] = jnp.zeros((lines, reach), jnp.bfloat16)
    tail = (pl.ds(blocks * lines, lines), pl.ds(BLOCK - reach, reach))
    ehigh[tail] = jnp.zeros((lines, reach), jnp.bfloat16)
    elow[tail] = jnp.zeros((lines, reach), jnp.bfloat16)

    def put(c, lane, x):
        high, low = split(x.reshape(lines, x.shape[2]))
        spot = (pl.ds(c * lines, lines), pl.ds(lane, x.shape[2]))
        ehigh[spot] = high
        elow[spot] = low

    def inner(step, carry):
        these = pl.ds(step * group, group)
        put(0, reach, vbuf[these, :, 0 : BLOCK - reach])
        for c in range(1, blocks):
            put(c, 0, vbuf[these, :, c * BLOCK - reach : (c + 1) * BLOCK - reach])
        put(blocks, 0, vbuf[these, :, width - reach : width])
        chunk = min(4, blocks)
        for c0 in range(0, blocks, chunk):
            here = pl.ds(c0 * lines, chunk * lines)
            there = pl.ds((c0 + 1) * lines, chunk * lines)
            h0, h1 = ehigh[here, :], ehigh[there, :]
            wide = jnp.concatenate([h0, h1, elow[here, :], elow[there, :], h0, h1], axis=1)
            res = jnp.dot(wide, table[...], preferred_element_type=jnp.float32)
            res = res.reshape(chunk, group, rows, BLOCK)
            for i in range(chunk):
                lane = (c0 + i) * BLOCK
                inner_ref[these, :, lane : lane + BLOCK] = res[i]
        return carry

    def finish_load(p, carry):
        load(p).wait()
        return carry

    for copy in table_loads:
        copy.wait()
    lax.fori_loop(0, group, finish_load, 0)
    inner(0, 0)
    lax.fori_loop(group, planes, finish_load, 0)

    def plane_sum(p, carry):
        x = vbuf[p]
        s = jnp.sum((x * x).reshape(rows // 8, 8, width), axis=0)
        acc = s[:, 0:128]
        for c in range(1, width // 128):
            acc = acc + s[:, c * 128 : (c + 1) * 128]
        part[pl.ds(p, 1), :] = jnp.sum(acc, axis=0, keepdims=True)
        return carry

    lax.fori_loop(0, planes, plane_sum, 0)

    row = lax.dot_general(
        jnp.ones((8, 128), jnp.float32), part[...], (((1,), (1,)), ((), ())), precision=HIGH
    )
    sums[0] = jnp.zeros((1, 128), jnp.float32)
    sums[0, :, 0:planes] = row[0:1]

    pl.semaphore_wait(barrier, nx * ny - 1)

    to_right = pltpu.make_async_remote_copy(
        src_ref=v_ref.at[:, :, pl.ds(width - reach, reach)],
        dst_ref=left_ref,
        send_sem=hsend.at[0],
        recv_sem=hrecv.at[0],
        device_id={"gx": lax.rem(gx + 1, nx)},
    )
    to_left = pltpu.make_async_remote_copy(
        src_ref=v_ref.at[:, :, pl.ds(0, reach)],
        dst_ref=right_ref,
        send_sem=hsend.at[1],
        recv_sem=hrecv.at[1],
        device_id={"gx": lax.rem(gx + nx - 1, nx)},
    )

    def give(d, carry):
        pltpu.make_async_remote_copy(
            src_ref=sums.at[0],
            dst_ref=sums.at[d],
            send_sem=ssend,
            recv_sem=srecv,
            device_id=partner(d),
        ).start()
        return carry

    lax.fori_loop(1, nx * ny, give, 0)

    @pl.when(jnp.logical_not(last))
    def _():
        to_right.start()

    @pl.when(jnp.logical_not(first))
    def _():
        to_left.start()

    sel_row = lax.broadcasted_iota(jnp.int32, (PACK, reach), 0)
    sel_col = lax.broadcasted_iota(jnp.int32, (PACK, reach), 1)

    def pack(lane, offset):
        pick = jnp.where((sel_row < depth) & (sel_col == sel_row + offset), 1.0, 0.0)
        tile = vbuf[:, :, lane : lane + reach].reshape(planes * rows, reach)
        return lax.dot_general(
            pick.astype(jnp.float32), tile, (((1,), (1,)), ((), ())), precision=HIGH
        )

    ends_out = pltpu.make_async_remote_copy(
        src_ref=ends.at[0], dst_ref=ends.at[0], send_sem=esend.at[0],
        recv_sem=erecv.at[0], device_id={"gx": nx - 1},
    )
    ends_back = pltpu.make_async_remote_copy(
        src_ref=ends.at[1], dst_ref=ends.at[1], send_sem=esend.at[1],
        recv_sem=erecv.at[1], device_id={"gx": 0},
    )

    @pl.when(first)
    def _():
        ends[0] = pack(0, 0)
        ends_out.start()

    @pl.when(last)
    def _():
        ends[1] = pack(width - reach, reach - depth)
        ends_back.start()

    lax.fori_loop(1, planes // group, inner, 0)

    @pl.when(first)
    def _():
        ends_out.wait_send()
        ends_back.wait_recv()

    @pl.when(last)
    def _():
        ends_back.wait_send()
        ends_out.wait_recv()

    others = sums.at[pl.ds(1, nx * ny - 1)]
    pltpu.make_async_copy(others, others, ssend).wait()
    pltpu.make_async_copy(others, others, srecv).wait()
    total_ref[...] = jnp.sum(sums[...], axis=0)

    @pl.when(jnp.logical_not(last))
    def _():
        to_right.wait_send()
        to_left.wait_recv()

    @pl.when(jnp.logical_not(first))
    def _():
        to_left.wait_send()
        to_right.wait_recv()


def exchange(velocity, table, reach, depth, nx, ny):
    planes, rows, width = velocity.shape
    group = min(4, planes)
    lines = group * rows
    blocks = width // BLOCK
    halo = jax.ShapeDtypeStruct((planes, rows, reach), jnp.float32)
    ends = jax.ShapeDtypeStruct((2, PACK, planes * rows), jnp.float32)
    total = jax.ShapeDtypeStruct((1, 128), jnp.float32)
    whole = jax.ShapeDtypeStruct(velocity.shape, jnp.float32)
    dma = pltpu.SemaphoreType.DMA
    vmem = pl.BlockSpec(memory_space=pltpu.VMEM)
    hbm = pl.BlockSpec(memory_space=pltpu.HBM)
    return pl.pallas_call(
        functools.partial(exchange_kernel, nx, ny, depth),
        out_shape=(halo, halo, ends, total, whole, whole),
        in_specs=[hbm, hbm],
        out_specs=(vmem,) * 6,
        scratch_shapes=[
            pltpu.VMEM(((blocks + 1) * lines, BLOCK), jnp.bfloat16),
            pltpu.VMEM(((blocks + 1) * lines, BLOCK), jnp.bfloat16),
            pltpu.VMEM((3 * (BLOCK + 2 * reach), BLOCK), table.dtype),
            pltpu.VMEM((nx * ny, 1, 128), jnp.float32),
            pltpu.VMEM((planes, 128), jnp.float32),
            dma((planes,)),
            dma,
            dma,
            dma((2,)),
            dma((2,)),
            dma((2,)),
            dma((2,)),
            dma((3,)),
        ],
        compiler_params=pltpu.CompilerParams(
            collective_id=0, has_side_effects=True, vmem_limit_bytes=38 * 2**20
        ),
        name="exchange",
    )(velocity, table)


def finish_kernel(
    nx, count, left_ref, right_ref, ends_ref, bl_ref, br_ref, tleft_ref, tright_ref,
    total_ref, inj_ref, v_ref, inner_ref, dudx_ref, rhs_ref,
    halo, blend, near, far, rbuf, isem, nsem, rsem,
):
    planes, rows, width = v_ref.shape
    reach = left_ref.shape[2]
    depth = bl_ref.shape[0]
    lines = planes * rows
    gx = lax.axis_index("gx")
    middle = pl.ds(reach, width - 2 * reach)

    def inside(p):
        return pltpu.make_async_copy(
            inner_ref.at[p, :, middle], dudx_ref.at[p, :, middle], isem.at[p]
        )

    for p in range(planes):
        inside(p).start()

    def continuation():
        blend[...] = jnp.zeros_like(blend)
        blend[0, 0:depth, :] = bl_ref[...]
        blend[1, 0:depth, :] = br_ref[...]
        return lax.dot_general(
            ends_ref[...].reshape(2 * PACK, lines),
            blend[...].reshape(2 * PACK, reach),
            (((0,), (0,)), ((), ())),
            precision=HIGH,
        )

    def edge(halo_ref, own, weight_ref, lane, result):
        @pl.when(own)
        def _():
            halo[...] = continuation()

        @pl.when(jnp.logical_not(own))
        def _():
            halo[...] = halo_ref[...].reshape(lines, reach)

        high, low = split(halo[...])
        wide = jnp.concatenate([high, low, high], axis=1)
        res = jnp.dot(wide, weight_ref[...], preferred_element_type=jnp.float32)
        result[...] = inner_ref[:, :, lane : lane + reach] + res.reshape(planes, rows, reach)

    edge(left_ref, gx == 0, tleft_ref, 0, near)
    put_near = pltpu.make_async_copy(near, dudx_ref.at[:, :, pl.ds(0, reach)], nsem.at[0])
    put_near.start()
    edge(right_ref, gx == nx - 1, tright_ref, width - reach, far)
    put_far = pltpu.make_async_copy(
        far, dudx_ref.at[:, :, pl.ds(width - reach, reach)], nsem.at[1]
    )
    put_far.start()

    place = lax.broadcasted_iota(jnp.int32, (1, 128), 1)
    total = total_ref[...]

    def put_rhs(p):
        return pltpu.make_async_copy(rbuf.at[p], rhs_ref.at[p], rsem.at[p])

    def plane(p, carry):
        here = jnp.sum(jnp.where(place == p, total, 0.0), axis=1, keepdims=True)
        forcing = inj_ref[p] / (here / count)
        low, high = pl.ds(0, reach), pl.ds(width - reach, reach)
        rbuf[p, :, low] = v_ref[p, :, low] * (forcing - near[p])
        rbuf[p, :, middle] = v_ref[p, :, middle] * (forcing - inner_ref[p, :, middle])
        rbuf[p, :, high] = v_ref[p, :, high] * (forcing - far[p])
        put_rhs(p).start()
        return carry

    lax.fori_loop(0, planes, plane, 0)
    for p in range(planes):
        inside(p).wait()
    put_near.wait()
    put_far.wait()
    for p in range(planes):
        put_rhs(p).wait()


def finish(nx, count, velocity, inner, left, right, ends, blends, total, injection, tables):
    planes, rows, width = velocity.shape
    reach = left.shape[2]
    whole = jax.ShapeDtypeStruct(velocity.shape, jnp.float32)
    vmem = pl.BlockSpec(memory_space=pltpu.VMEM)
    hbm = pl.BlockSpec(memory_space=pltpu.HBM)
    dma = pltpu.SemaphoreType.DMA
    strip = pltpu.VMEM((planes, rows, reach), jnp.float32)
    return pl.pallas_call(
        functools.partial(finish_kernel, nx, count),
        out_shape=(whole, whole),
        in_specs=[vmem] * 8 + [pl.BlockSpec(memory_space=pltpu.SMEM)] + [vmem] * 2,
        out_specs=(hbm, hbm),
        scratch_shapes=[
            pltpu.VMEM((planes * rows, reach), jnp.float32),
            pltpu.VMEM((2, PACK, reach), jnp.float32),
            strip,
            strip,
            pltpu.VMEM(velocity.shape, jnp.float32),
            dma((planes,)),
            dma((2,)),
            dma((planes,)),
        ],
        compiler_params=pltpu.CompilerParams(vmem_limit_bytes=36 * 2**20),
        name="finish",
    )(left, right, ends, *blends, *tables, total, injection, velocity, inner)


def per_device(nx, ny, velocity, blend_left, blend_right, injection):
    planes, rows, width = velocity.shape
    reach = blend_left.shape[0]
    period = width * nx + reach
    count = width * nx * rows * ny
    high, low = toeplitz(period, reach)
    table = jnp.asarray(np.concatenate([high, low], axis=0))
    head, foot = slice(0, reach), slice(BLOCK + reach, None)
    near, far = slice(0, reach), slice(BLOCK - reach, None)
    tleft = jnp.asarray(np.concatenate([high[head, near], high[head, near], low[head, near]]))
    tright = jnp.asarray(np.concatenate([high[foot, far], high[foot, far], low[foot, far]]))
    left, right, ends, total, points, inner = exchange(
        velocity, table, reach, blend_left.shape[1], nx, ny
    )
    blends = (blend_left.T, blend_right.T)
    return finish(
        nx, count, points, inner, left, right, ends, blends, total, injection, (tleft, tright)
    )


def solution(mesh):
    placed = (P(None, "gy", "gx"), P(), P(), P())
    return jax.shard_map(
        functools.partial(per_device, mesh.shape["gx"], mesh.shape["gy"]),
        mesh=mesh,
        in_specs=placed,
        out_specs=(P(None, "gy", "gx"), P(None, "gy", "gx")),
        check_vma=False,
    )
```
